256 devices in a mesh: gx: 16 (over z_hi, y), gy: 16 (over z_lo, x, core).
Axes of the slice: x: 4, y: 4, z: 8 (z_hi: 4, z_lo: 2; z = z_hi * 2 + z_lo), core: 2. Of those that a mesh axis runs over, the one named last changes fastest.
Arguments:
- modes: bfloat16 [256, 256, 2, 3, 128], P('gx', 'gy'), may hold values from -8 to 8
Outputs:
- convective: float32 [128, 128, 128], P('gx', 'gy')
- viscous: float32 [128, 128], P('gx', 'gy')
The draws below stay inside these ranges and needn't reach their ends.
All inputs are finite; a program needn't handle non-finite values.
Results may differ from the reference program's by a relative error of at most 0.004.
Values may be sent and summed in bfloat16 or wider, within the bound.
A program may use at most 64 MiB of HBM per device.

```python
import math
import jax
import jax.numpy as jnp
from jax import lax

M = 128
CZ = 2
NX = 256
NY = 256
NTOT = 131072


def draw_modes(key, part):
    base = jax.random.fold_in(key, 11)
    key_white, key_mix = jax.random.split(base, 2)
    rows_all = NX * NY * CZ * 3
    white = jax.random.normal(key_white, (rows_all, M), jnp.float32)
    mixing = jax.random.normal(key_mix, (M, M), jnp.float32) / math.sqrt(M)
    mixed = jnp.dot(white, mixing, precision=lax.Precision.HIGHEST)
    mixed = jnp.clip(mixed, -8.0, 8.0)
    return mixed.reshape(NX, NY, CZ, 3, M).astype(jnp.bfloat16)


def setup_inputs(seed: int = 0) -> dict:
    key_of = jax.random.split(jax.random.key(seed), 2)
    return {
        "modes": draw_modes(jax.random.fold_in(key_of[1], 71), 0),
    }


def fourth(padded, axis, count):

    def cut(offset):
        return lax.slice_in_dim(padded, 2 + offset, 2 + offset + count, axis=axis)
    return (8.0 * (cut(1) - cut(-1)) - (cut(2) - cut(-2))) / 12.0

def reference(modes):
    field = modes.astype(jnp.float32)
    zero_pads = [(0, 0)] * 5
    pads_x = list(zero_pads)
    pads_x[0] = (2, 2)
    pads_y = list(zero_pads)
    pads_y[1] = (2, 2)
    pads_z = list(zero_pads)
    pads_z[2] = (2, 2)
    grad_x = fourth(jnp.pad(field, pads_x, mode='wrap'), 0, NX)
    grad_y = fourth(jnp.pad(field, pads_y, mode='wrap'), 1, NY)
    grad_z = fourth(jnp.pad(field, pads_z), 2, CZ)
    gradient = jnp.stack([grad_x, grad_y, grad_z]).astype(jnp.bfloat16)
    flat_modes = modes.reshape(NTOT, 3, M)
    flat_grad = gradient.reshape(3, NTOT, 3, M)
    stacked = gradient.reshape(-1, M)
    viscous = -lax.dot_general(stacked, stacked, (((0,), (0,)), ((), ())), preferred_element_type=jnp.float32) / NTOT
    block_pts = math.gcd(NTOT, 2048)
    count_blocks = NTOT // block_pts

    def accumulate(total, index):
        start = (index * block_pts).astype(jnp.int32)
        phi_block = lax.dynamic_slice_in_dim(flat_modes, start, block_pts, 0).astype(jnp.float32)
        grad_block = lax.dynamic_slice_in_dim(flat_grad, start, block_pts, 1).astype(jnp.float32)
        pair = jnp.einsum('pai,bpak->ikbp', phi_block, grad_block).astype(jnp.bfloat16)
        right_side = phi_block.transpose(1, 0, 2).reshape(3 * block_pts, M).astype(jnp.bfloat16)
        term = jnp.dot(pair.reshape(M * M, 3 * block_pts), right_side, preferred_element_type=jnp.float32)
        return (total + term.reshape(M, M, M), None)
    total, _ = lax.scan(accumulate, jnp.zeros((M, M, M), jnp.float32), jnp.arange(count_blocks, dtype=jnp.int32))
    convective = -total / jnp.sqrt(jnp.float32(NTOT))
    return (convective, viscous)
```

```python
import functools
import math

import jax
import jax.numpy as jnp
import numpy as np
from jax import lax
from jax.experimental import pallas as pl
from jax.experimental.pallas import tpu as pltpu
from jax.sharding import PartitionSpec as P

F32 = jnp.float32
BF16 = jnp.bfloat16
MESH = pl.DeviceIdType.MESH

ROWS = 16


def stencil_matrix():
    def column(x, y):
        if x < 0:
            return 256 + (x + 2) * 16 + y
        if x > 15:
            return 288 + (x - 16) * 16 + y
        if y < 0:
            return 320 + x * 2 + y + 2
        if y > 15:
            return 352 + x * 2 + y - 16
        return x * 16 + y

    mat = np.zeros((512, 384), np.float32)
    for x in range(16):
        for y in range(16):
            for off, w in ((1, 8.0), (-1, -8.0), (2, -1.0), (-2, 1.0)):
                mat[x * 16 + y, column(x + off, y)] = w
                mat[256 + x * 16 + y, column(x, y + off)] = w
    return mat


def edge_matrix():
    mat = np.zeros((64, 256), np.float32)
    for side in range(2):
        for x in range(16):
            for l in range(2):
                mat[side * 32 + x * 2 + l, x * 16 + 14 * side + l] = 1.0
    return mat


def kernel(
    m_ref, d_ref, e_ref, i_ref, conv_ref, visc_ref,
    ext, ed, mf, mt, gbf, gt, w0, w1, acc, vacc,
    sx, sy, s2x, s2y, s3, r1x, r1y, r2x, r2y, r3,
    v1, v2, v3, rv1, rv2, rv3,
    hs, hr, x1s, x1r, y1s, y1r, x2s, x2r, y2s, y2r, zs, zr,
    v1s, v1r, v2s, v2r, v3s, v3r,
):
    gx, gy = lax.axis_index("gx"), lax.axis_index("gy")
    zh, yy = gx // 4, gx % 4
    zl, xx, cc = gy // 8, (gy // 2) % 4, gy % 2
    chip = gy // 2
    zz = zh * 2 + zl
    other = 1 - cc

    def at_x(d):
        return (gx, zl * 8 + ((xx + d) % 4) * 2 + cc)

    def at_y(d):
        return (zh * 4 + (yy + d) % 4, gy)

    def at_z(z):
        return ((z // 2) * 4 + yy, (z % 2) * 8 + xx * 2 + cc)

    def chip_core(step, core):
        return (gx, ((chip + 8 + step) % 8) * 2 + core)

    def row_core(step, core):
        return ((gx + 16 + step) % 16, chip * 2 + core)

    def put(src, dst, send, recv, dev):
        return pltpu.make_async_remote_copy(
            src_ref=src, dst_ref=dst, send_sem=send, recv_sem=recv,
            device_id=dev, device_id_type=MESH,
        )

    barrier = pltpu.get_barrier_semaphore()
    peers = [(gx, chip * 2 + other)]
    for core in range(2):
        for step in (-1, 1):
            peers.append(chip_core(step, core))
            peers.append(row_core(step, core))
    for d in range(1, 4):
        peers.append(at_x(d))
        peers.append(at_y(d))
    for d in range(1, 8):
        peers.append(at_z((zz + d) % 8))
    for dev in peers:
        pl.semaphore_signal(barrier, inc=1, device_id=dev, device_id_type=MESH)

    for za in range(6):
        slab = m_ref[za].reshape(256, 128)
        ext[cc, za, 0:8] = m_ref[za]
        edges = jnp.dot(e_ref[...], slab, preferred_element_type=F32).astype(BF16)
        ed[0, za] = edges[0:32]
        ed[1, za] = edges[32:64]
    for za in range(6):
        ext[other, za, 10 + cc] = ed[other, za]
    pl.semaphore_wait(barrier, len(peers))

    partner = (gx, chip * 2 + other)
    halo = [
        put(m_ref, ext.at[cc, :, 0:8], hs.at[0], hr.at[0], partner),
        put(ed.at[other], ext.at[other, :, 10 + cc], hs.at[1], hr.at[1], partner),
    ]
    for core in range(2):
        halo.append(put(m_ref.at[:, 7], ext.at[cc, :, 8], hs.at[2 + core], hr.at[2 + cc], row_core(1, core)))
        halo.append(put(m_ref.at[:, 0], ext.at[cc, :, 9], hs.at[4 + core], hr.at[4 + cc], row_core(-1, core)))
        halo.append(
            put(ed.at[cc], ext.at[other, :, 11 - cc], hs.at[6 + core], hr.at[6 + cc], chip_core(2 * cc - 1, core))
        )
    for copy in halo:
        copy.start()

    put(m_ref, ext.at[other, :, 0:8], hs.at[0], hr.at[0], partner).wait_recv()
    put(ed.at[cc], ext.at[cc, :, 10 + other], hs.at[1], hr.at[1], partner).wait_recv()
    for blk in range(2):
        put(m_ref.at[:, 7], ext.at[blk, :, 8], hs.at[2], hr.at[2 + blk], partner).wait_recv()
        put(m_ref.at[:, 0], ext.at[blk, :, 9], hs.at[4], hr.at[4 + blk], partner).wait_recv()
        put(ed.at[blk], ext.at[1 - blk, :, 11 - blk], hs.at[6], hr.at[6 + blk], partner).wait_recv()

    lane = lax.broadcasted_iota(jnp.int32, (32, 128), 1)
    mode_of = [16 * ((lane // 64) * 4 + x) + 8 * cc + lane % 8 for x in range(4)]

    def prepare(bz, _):
        blk, z = bz // 2, bz % 2
        sign = (1 - 2 * z).astype(F32) * (8.0 / 12.0)
        for a in range(3):
            whole = ext[blk, z * 3 + a].reshape(384, 128)
            slab = whole[0:256]
            mf[bz, a] = slab.astype(F32)
            mt[bz, :, a * 256 : a * 256 + 256] = lax.dot_general(
                i_ref[...], slab, (((1,), (1,)), ((), ())), preferred_element_type=F32
            ).astype(BF16)
            both = jnp.dot(d_ref[...], whole, preferred_element_type=F32) * (1.0 / 12.0)
            gbf[bz, 0, a] = both[0:256].astype(BF16)
            gbf[bz, 1, a] = both[256:512].astype(BF16)
            along_z = ext[blk, (1 - z) * 3 + a, 0:8].reshape(256, 128).astype(F32) * sign
            gbf[bz, 2, a] = along_z.astype(BF16)
        for a in range(3):
            for b in range(3):
                for p in range(0, 256, 32):
                    part = gbf[bz, b, a, p : p + 32].astype(F32)
                    for x in range(4):
                        gt[bz, b, a, p : p + 32, x * 128 : x * 128 + 128] = jnp.take_along_axis(
                            part, mode_of[x], axis=1
                        )
        return 0

    lax.fori_loop(0, 4, prepare, 0)

    vacc[...] = jnp.zeros_like(vacc)

    def viscous(bz, _):
        total = vacc[...]
        for b in range(3):
            for a in range(3):
                g = gbf[bz, b, a]
                total += lax.dot_general(g, g, (((0,), (0,)), ((), ())), preferred_element_type=F32)
        vacc[...] = total
        return 0

    lax.fori_loop(0, 4, viscous, 0)
    for h in range(4):
        for y in range(4):
            v1[y, h] = vacc[(h * 4 + y) * 8 : (h * 4 + y) * 8 + 8, :]
    for d in range(1, 4):
        put(v1.at[(yy + d) % 4], rv1.at[d - 1], v1s.at[d - 1], v1r.at[d - 1], at_y(d)).start()

    ws = (w0, w1)
    lane16 = lax.broadcasted_iota(jnp.int32, (16, 128), 1)

    def products(it, bz):
        zi, tp = it // 2, it % 2
        zt = (zh + 1 + zi) % 4
        idx = [
            (lane16 % 64) // 8 + 8 * (zt * 4 + (yy + 1 + 2 * tp + e) % 4) for e in range(2)
        ]
        w = ws[bz % 2]
        for p in range(0, 256, 16):
            left = [
                [jnp.take_along_axis(mf[bz, a, p : p + 16], idx[e], axis=1) for a in range(3)]
                for e in range(2)
            ]
            for b in range(3):
                for x in range(4):
                    g = [gt[bz, b, a, p : p + 16, x * 128 : x * 128 + 128] for a in range(3)]
                    pair = [
                        left[e][0] * g[0] + left[e][1] * g[1] + left[e][2] * g[2] for e in range(2)
                    ]
                    w[b * 256 + p : b * 256 + p + 16, x * 256 : x * 256 + 256] = jnp.concatenate(
                        pair, axis=1
                    ).astype(BF16)

    def project(bz):
        w = ws[bz % 2]
        for x in range(4):
            cols = slice(x * 256, x * 256 + 256)
            term = jnp.dot(mt[bz], w[:, cols], preferred_element_type=F32)
            if bz == 0:
                acc[:, cols] = term
            else:
                acc[:, cols] += term

    def send_first(it):
        for e in range(2):
            n = it * 2 + e
            for x in range(4):
                tile = acc[:, x * 256 + e * 128 : x * 256 + e * 128 + 128].astype(BF16)
                sx[n, x] = tile[0:64]
                sy[n, x] = tile[64:128]
            for d in range(1, 4):
                put(sx.at[n, (xx + d) % 4], r1x.at[n, d - 1], x1s.at[n, d - 1], x1r.at[n, d - 1], at_x(d)).start()
        zi, tp = it // 2, it % 2
        n = it * 2
        put(sy.at[n], r1y.at[zi, 2 * tp], y1s.at[n], y1r.at[zi, 2 * tp], at_y(1 + 2 * tp)).start()

        @pl.when(tp == 0)
        def _():
            put(sy.at[n + 1], r1y.at[zi, 1], y1s.at[n + 1], y1r.at[zi, 1], at_y(2)).start()

    def x_first(it):
        zi, tp = it // 2, it % 2
        for e in range(2):
            n = it * 2 + e
            for d in range(1, 4):
                put(sx.at[n, 0], r1x.at[n, d - 1], x1s.at[n, d - 1], x1r.at[n, d - 1], at_x(d)).wait_recv()
            total = sx[n, xx].astype(F32)
            for d in range(3):
                total += r1x[n, d].astype(F32)
            s2x[n] = total.astype(BF16)
        n = it * 2
        put(s2x.at[n], r2x.at[zi, 2 * tp], x2s.at[n], x2r.at[zi, 2 * tp], at_y(1 + 2 * tp)).start()

        @pl.when(tp == 0)
        def _():
            put(s2x.at[n + 1], r2x.at[zi, 1], x2s.at[n + 1], x2r.at[zi, 1], at_y(2)).start()

    def y_first(zi):
        for d in range(3):
            put(sy.at[0], r1y.at[zi, d], y1s.at[0], y1r.at[zi, d], at_y(d + 1)).wait_recv()
        for x in range(4):
            total = sy[zi * 4 + 3, x].astype(F32)
            for d in range(3):
                total += r1y[zi, d, x].astype(F32)
            s2y[zi, x] = total.astype(BF16)
        for d in range(1, 4):
            put(s2y.at[zi, (xx + d) % 4], r2y.at[zi, d - 1], y2s.at[zi, d - 1], y2r.at[zi, d - 1], at_x(d)).start()

    def second(zi):
        for d in range(3):
            put(s2x.at[0], r2x.at[zi, d], x2s.at[0], x2r.at[zi, d], at_y(d + 1)).wait_recv()
        for d in range(3):
            put(s2y.at[0, 0], r2y.at[zi, d], y2s.at[0, 0], y2r.at[zi, d], at_x(d + 1)).wait_recv()
        upper = s2x[zi * 4 + 3].astype(F32)
        lower = s2y[zi, xx].astype(F32)
        for d in range(3):
            upper += r2x[zi, d].astype(F32)
            lower += r2y[zi, d].astype(F32)
        turned = jnp.concatenate([upper, lower], axis=0).T
        s3[zi, 0] = turned[0:64]
        s3[zi, 1] = turned[64:128]
        zt = (zh + 1 + zi) % 4
        for l in range(2):
            dst = zt * 2 + l
            dist = (dst - zz + 8) % 8

            @pl.when(dist != 0)
            def _():
                put(s3.at[zi, l], r3.at[dist - 1], zs.at[zi, l], zr.at[dist - 1], at_z(dst)).start()

    def visc_second():
        for d in range(1, 4):
            put(v1.at[0], rv1.at[d - 1], v1s.at[d - 1], v1r.at[d - 1], at_y(d)).wait_recv()
        v2[...] = v1[yy] + rv1[0] + rv1[1] + rv1[2]
        for d in range(1, 4):
            put(v2, rv2.at[d - 1], v2s.at[d - 1], v2r.at[d - 1], at_x(d)).start()

    def visc_third():
        for d in range(1, 4):
            put(v2, rv2.at[d - 1], v2s.at[d - 1], v2r.at[d - 1], at_x(d)).wait_recv()
        v3[...] = v2[...] + rv2[0] + rv2[1] + rv2[2]
        for d in range(1, 8):
            z = (zz + d) % 8
            put(v3.at[z // 2], rv3.at[d - 1], v3s.at[d - 1], v3r.at[d - 1], at_z(z)).start()

    def step(it, _):
        products(it, 0)
        for bz in range(1, 4):
            products(it, bz)
            project(bz - 1)
        project(3)
        send_first(it)

        @pl.when(it >= 1)
        def _():
            x_first(it - 1)

        @pl.when((it >= 2) & (it % 2 == 0))
        def _():
            y_first(it // 2 - 1)

        @pl.when((it >= 3) & (it % 2 == 1))
        def _():
            second(it // 2 - 1)

        @pl.when(it == 1)
        def _():
            visc_second()

        @pl.when(it == 3)
        def _():
            visc_third()

        return 0

    lax.fori_loop(0, 8, step, 0)
    x_first(7)
    y_first(3)
    second(3)

    points = 131072.0
    vtotal = v3[zh]
    for d in range(1, 8):
        put(v3.at[0], rv3.at[d - 1], v3s.at[d - 1], v3r.at[d - 1], partner).wait_recv()
        vtotal += rv3[d - 1]
    lane8 = lax.broadcasted_iota(jnp.int32, (8, 128), 1)
    own = jnp.take_along_axis(vtotal, (lane8 + 8 * gy) % 128, axis=1)
    visc_ref[...] = own[:, 0:8] * (-1.0 / points)
    total = s3[3, zl]
    for d in range(1, 8):
        put(s3.at[0, 0], r3.at[d - 1], zs.at[0, 0], zr.at[d - 1], partner).wait_recv()
        total += r3[d - 1]
    conv_ref[...] = (total * (-1.0 / math.sqrt(points))).reshape(8, 8, 128)

    for copy in halo:
        copy.wait_send()
    for d in range(3):
        put(v1.at[0], rv1.at[d], v1s.at[d], v1r.at[d], partner).wait_send()
        put(v2, rv2.at[d], v2s.at[d], v2r.at[d], partner).wait_send()
    for d in range(7):
        put(v3.at[0], rv3.at[d], v3s.at[d], v3r.at[d], partner).wait_send()

    def sent(zi, _):
        for t in range(4):
            n = zi * 4 + t
            for d in range(3):
                put(sx.at[n, 0], r1x.at[n, d], x1s.at[n, d], x1r.at[n, d], partner).wait_send()
            if t < 3:
                put(sy.at[n], r1y.at[zi, t], y1s.at[n], y1r.at[zi, t], partner).wait_send()
                put(s2x.at[n], r2x.at[zi, t], x2s.at[n], x2r.at[zi, t], partner).wait_send()
        for d in range(3):
            put(s2y.at[zi, 0], r2y.at[zi, d], y2s.at[zi, d], y2r.at[zi, d], partner).wait_send()
        zt = (zh + 1 + zi) % 4
        for l in range(2):

            @pl.when(zt * 2 + l != zz)
            def _():
                put(s3.at[zi, l], r3.at[0], zs.at[zi, l], zr.at[0], partner).wait_send()

        return 0

    lax.fori_loop(0, 4, sent, 0)


def body(modes):
    slabs = modes.transpose(2, 3, 0, 1, 4).reshape(6, 8, 32, 128)
    stencil = jnp.asarray(stencil_matrix(), BF16)
    edges = jnp.asarray(edge_matrix(), BF16)
    eye = jnp.eye(128, dtype=BF16)
    dma = pltpu.SemaphoreType.DMA
    vmem = pltpu.VMEM
    return pl.pallas_call(
        kernel,
        out_shape=(
            jax.ShapeDtypeStruct((8, 8, 128), F32),
            jax.ShapeDtypeStruct((8, 8), F32),
        ),
        in_specs=[pl.BlockSpec(memory_space=vmem)] * 4,
        out_specs=(pl.BlockSpec(memory_space=vmem),) * 2,
        scratch_shapes=[
            vmem((2, 6, 12, 32, 128), BF16),
            vmem((2, 6, 32, 128), BF16),
            vmem((4, 3, 256, 128), F32),
            vmem((4, 128, 768), BF16),
            vmem((4, 3, 3, 256, 128), BF16),
            vmem((4, 3, 3, 256, 512), F32),
            vmem((768, 1024), BF16),
            vmem((768, 1024), BF16),
            vmem((128, 1024), F32),
            vmem((128, 128), F32),
            vmem((16, 4, 64, 128), BF16),
            vmem((16, 4, 64, 128), BF16),
            vmem((16, 64, 128), BF16),
            vmem((4, 4, 64, 128), BF16),
            vmem((4, 2, 64, 128), F32),
            vmem((16, 3, 64, 128), BF16),
            vmem((4, 3, 4, 64, 128), BF16),
            vmem((4, 3, 64, 128), BF16),
            vmem((4, 3, 64, 128), BF16),
            vmem((7, 64, 128), F32),
            vmem((4, 4, 8, 128), F32),
            vmem((4, 8, 128), F32),
            vmem((4, 8, 128), F32),
            vmem((3, 4, 8, 128), F32),
            vmem((3, 4, 8, 128), F32),
            vmem((7, 8, 128), F32),
            dma((8,)), dma((8,)),
            dma((16, 3)), dma((16, 3)),
            dma((16,)), dma((4, 3)),
            dma((16,)), dma((4, 3)),
            dma((4, 3)), dma((4, 3)),
            dma((4, 2)), dma((7,)),
            dma((3,)), dma((3,)),
            dma((3,)), dma((3,)),
            dma((7,)), dma((7,)),
        ],
        compiler_params=pltpu.CompilerParams(
            collective_id=0, has_side_effects=True, vmem_limit_bytes=60 * 2**20
        ),
    )(slabs, stencil, edges, eye)


def solution(mesh):
    in_specs = (P("gx", "gy", None, None, None),)
    out_specs = (P("gx", "gy", None), P("gx", "gy"))
    return jax.shard_map(body, mesh=mesh, in_specs=in_specs, out_specs=out_specs, check_vma=False)
```

```python
import functools
import math

import jax
import jax.numpy as jnp
import numpy as np
from jax import lax
from jax.experimental import pallas as pl
from jax.experimental.pallas import tpu as pltpu
from jax.sharding import PartitionSpec as P

F32 = jnp.float32
BF16 = jnp.bfloat16
MESH = pl.DeviceIdType.MESH

ROWS = 16


def stencil_matrix():
    def column(x, y):
        if x < 0:
            return 256 + (x + 2) * 16 + y
        if x > 15:
            return 288 + (x - 16) * 16 + y
        if y < 0:
            return 320 + x * 2 + y + 2
        if y > 15:
            return 352 + x * 2 + y - 16
        return x * 16 + y

    mat = np.zeros((512, 384), np.float32)
    for x in range(16):
        for y in range(16):
            for off, w in ((1, 8.0), (-1, -8.0), (2, -1.0), (-2, 1.0)):
                mat[x * 16 + y, column(x + off, y)] = w
                mat[256 + x * 16 + y, column(x, y + off)] = w
    return mat


def edge_matrix():
    mat = np.zeros((64, 256), np.float32)
    for side in range(2):
        for x in range(16):
            for l in range(2):
                mat[side * 32 + x * 2 + l, x * 16 + 14 * side + l] = 1.0
    return mat


def kernel(
    m_hbm, d_hbm, e_hbm, i_hbm, conv_ref, visc_ref,
    d_ref, e_ref, i_ref, ext, ed, mf, mt, gbf, gt, w0, w1, acc, vacc,
    sx, sy, s2x, s2y, s3, r1x, r1y, r2x, r2y, r3,
    v1, v2, v3, rv1, rv2, rv3,
    hs, hr, x1s, x1r, y1s, y1r, x2s, x2r, y2s, y2r, zs, zr,
    v1s, v1r, v2s, v2r, v3s, v3r, ins, rv0, v0s, v0r, pick,
):
    gx, gy = lax.axis_index("gx"), lax.axis_index("gy")
    zh, yy = gx // 4, gx % 4
    zl, xx, cc = gy // 8, (gy // 2) % 4, gy % 2
    chip = gy // 2
    zz = zh * 2 + zl
    other = 1 - cc

    def at_x(d):
        return (gx, zl * 8 + ((xx + d) % 4) * 2 + cc)

    def at_y(d):
        return (zh * 4 + (yy + d) % 4, gy)

    def at_z(z):
        return ((z // 2) * 4 + yy, (z % 2) * 8 + xx * 2 + cc)

    def chip_core(step, core):
        return (gx, ((chip + 8 + step) % 8) * 2 + core)

    def row_core(step, core):
        return ((gx + 16 + step) % 16, chip * 2 + core)

    def put(src, dst, send, recv, dev):
        return pltpu.make_async_remote_copy(
            src_ref=src, dst_ref=dst, send_sem=send, recv_sem=recv,
            device_id=dev, device_id_type=MESH,
        )

    barrier = pltpu.get_barrier_semaphore()
    peers = [(gx, chip * 2 + other)]
    for core in range(2):
        for step in (-1, 1):
            peers.append(chip_core(step, core))
            peers.append(row_core(step, core))
    for d in range(1, 4):
        peers.append(at_x(d))
        peers.append(at_y(d))
    for d in range(1, 8):
        peers.append(at_z((zz + d) % 8))
    for dev in peers:
        pl.semaphore_signal(barrier, inc=1, device_id=dev, device_id_type=MESH)

    loads = [
        pltpu.make_async_copy(m_hbm, ext.at[cc, :, 0:8], ins.at[0]),
        pltpu.make_async_copy(e_hbm, e_ref, ins.at[1]),
        pltpu.make_async_copy(i_hbm, i_ref, ins.at[2]),
        pltpu.make_async_copy(d_hbm, d_ref, ins.at[3]),
    ]
    for copy in loads:
        copy.start()
    loads[1].wait()
    loads[0].wait()
    for za in range(6):
        slab = ext[cc, za, 0:8].reshape(256, 128)
        edges = jnp.dot(e_ref[...], slab, preferred_element_type=F32).astype(BF16)
        ed[0, za] = edges[0:32]
        ed[1, za] = edges[32:64]
    for za in range(6):
        ext[other, za, 10 + cc] = ed[other, za]
    pl.semaphore_wait(barrier, len(peers))

    partner = (gx, chip * 2 + other)
    mine = ext.at[cc, :, 0:8]
    last, first = ext.at[cc, :, 7], ext.at[cc, :, 0]
    halo = [
        put(mine, ext.at[cc, :, 0:8], hs.at[0], hr.at[0], partner),
        put(ed.at[other], ext.at[other, :, 10 + cc], hs.at[1], hr.at[1], partner),
    ]
    for core in range(2):
        halo.append(put(last, ext.at[cc, :, 8], hs.at[2 + core], hr.at[2 + cc], row_core(1, core)))
        halo.append(put(first, ext.at[cc, :, 9], hs.at[4 + core], hr.at[4 + cc], row_core(-1, core)))
        halo.append(
            put(ed.at[cc], ext.at[other, :, 11 - cc], hs.at[6 + core], hr.at[6 + cc], chip_core(2 * cc - 1, core))
        )
    for copy in halo:
        copy.start()

    lane = lax.broadcasted_iota(jnp.int32, (32, 128), 1)
    mode_of = [16 * ((lane // 64) * 4 + x) + 8 * cc + lane % 8 for x in range(4)]
    row128 = lax.broadcasted_iota(jnp.int32, (128, 128), 0)
    lane128 = lax.broadcasted_iota(jnp.int32, (128, 128), 1)
    for x in range(2):
        wanted = 16 * ((lane128 // 64) * 4 + x) + 8 * cc + lane128 % 8
        pick[:, x * 128 : x * 128 + 128] = jnp.where(row128 == wanted, 1.0, 0.0).astype(BF16)

    def expand(bz, b, a):
        gt[bz, b, a, :, 0:256] = jnp.dot(gbf[bz, b, a], pick[...], preferred_element_type=F32)
        for p in range(0, 256, 32):
            part = gbf[bz, b, a, p : p + 32].astype(F32)
            for x in range(2, 4):
                gt[bz, b, a, p : p + 32, x * 128 : x * 128 + 128] = jnp.take_along_axis(
                    part, mode_of[x], axis=1
                )

    def inner(blk):
        def one(z, _):
            bz = blk * 2 + z
            sign = (1 - 2 * z).astype(F32) * (8.0 / 12.0)
            for a in range(3):
                slab = ext[blk, z * 3 + a, 0:8].reshape(256, 128)
                mf[bz, a] = slab.astype(F32)
                mt[bz, :, a * 256 : a * 256 + 256] = lax.dot_general(
                    i_ref[...], slab, (((1,), (1,)), ((), ())), preferred_element_type=F32
                ).astype(BF16)
                along_z = ext[blk, (1 - z) * 3 + a, 0:8].reshape(256, 128).astype(F32) * sign
                gbf[bz, 2, a] = along_z.astype(BF16)
            for a in range(3):
                expand(bz, 2, a)
            return 0

        lax.fori_loop(0, 2, one, 0)

    def outer(blk):
        def one(z, _):
            bz = blk * 2 + z
            for a in range(3):
                whole = ext[blk, z * 3 + a].reshape(384, 128)
                both = jnp.dot(d_ref[...], whole, preferred_element_type=F32) * (1.0 / 12.0)
                gbf[bz, 0, a] = both[0:256].astype(BF16)
                gbf[bz, 1, a] = both[256:512].astype(BF16)
            for a in range(3):
                for b in range(2):
                    expand(bz, b, a)
            return 0

        lax.fori_loop(0, 2, one, 0)

    def rows_in(blk):
        put(last, ext.at[blk, :, 8], hs.at[2], hr.at[2 + blk], partner).wait_recv()
        put(first, ext.at[blk, :, 9], hs.at[4], hr.at[4 + blk], partner).wait_recv()
        put(ed.at[0], ext.at[blk, :, 10 + blk], hs.at[6], hr.at[7 - blk], partner).wait_recv()

    loads[2].wait()
    inner(cc)
    put(mine, ext.at[other, :, 0:8], hs.at[0], hr.at[0], partner).wait_recv()
    inner(other)
    loads[3].wait()
    put(ed.at[cc], ext.at[cc, :, 10 + other], hs.at[1], hr.at[1], partner).wait_recv()
    rows_in(cc)
    outer(cc)
    rows_in(other)
    outer(other)

    vacc[...] = jnp.zeros_like(vacc)

    def viscous(it):
        bz = cc * 2 + it
        total = vacc[...]
        for b in range(3):
            for a in range(3):
                g = gbf[bz, b, a]
                total += lax.dot_general(g, g, (((0,), (0,)), ((), ())), preferred_element_type=F32)
        vacc[...] = total

    def visc_pair():
        return put(vacc, rv0, v0s.at[0], v0r.at[0], partner)

    def visc_first():
        visc_pair().wait_recv()
        for h in range(4):
            for y in range(4):
                rows = slice((h * 4 + y) * 8, (h * 4 + y) * 8 + 8)
                v1[y, h] = vacc[rows, :] + rv0[rows, :]
        for d in range(1, 4):
            put(v1.at[(yy + d) % 4], rv1.at[d - 1], v1s.at[d - 1], v1r.at[d - 1], at_y(d)).start()

    ws = (w0, w1)
    lane16 = lax.broadcasted_iota(jnp.int32, (16, 128), 1)

    def products(it, bz):
        zi, tp = it // 2, it % 2
        zt = (zh + 1 + zi) % 4
        idx = [
            (lane16 % 64) // 8 + 8 * (zt * 4 + (yy + 1 + 2 * tp + e) % 4) for e in range(2)
        ]
        w = ws[bz % 2]
        for p in range(0, 256, 16):
            left = [
                [jnp.take_along_axis(mf[bz, a, p : p + 16], idx[e], axis=1) for a in range(3)]
                for e in range(2)
            ]
            for b in range(3):
                for x in range(4):
                    g = [gt[bz, b, a, p : p + 16, x * 128 : x * 128 + 128] for a in range(3)]
                    pair = [
                        left[e][0] * g[0] + left[e][1] * g[1] + left[e][2] * g[2] for e in range(2)
                    ]
                    w[b * 256 + p : b * 256 + p + 16, x * 256 : x * 256 + 256] = jnp.concatenate(
                        pair, axis=1
                    ).astype(BF16)

    def project(bz):
        w = ws[bz % 2]
        for x in range(4):
            cols = slice(x * 256, x * 256 + 256)
            term = jnp.dot(mt[bz], w[:, cols], preferred_element_type=F32)
            if bz == 0:
                acc[:, cols] = term
            else:
                acc[:, cols] += term

    def send_first(it):
        for e in range(2):
            n = it * 2 + e
            for x in range(4):
                tile = acc[:, x * 256 + e * 128 : x * 256 + e * 128 + 128].astype(BF16)
                sx[n, x] = tile[0:64]
                sy[n, x] = tile[64:128]
            for d in range(1, 4):
                put(sx.at[n, (xx + d) % 4], r1x.at[n, d - 1], x1s.at[n, d - 1], x1r.at[n, d - 1], at_x(d)).start()
        zi, tp = it // 2, it % 2
        n = it * 2
        put(sy.at[n], r1y.at[zi, 2 * tp], y1s.at[n], y1r.at[zi, 2 * tp], at_y(1 + 2 * tp)).start()

        @pl.when(tp == 0)
        def _():
            put(sy.at[n + 1], r1y.at[zi, 1], y1s.at[n + 1], y1r.at[zi, 1], at_y(2)).start()

    def x_first(it):
        zi, tp = it // 2, it % 2
        for e in range(2):
            n = it * 2 + e
            for d in range(1, 4):
                put(sx.at[n, 0], r1x.at[n, d - 1], x1s.at[n, d - 1], x1r.at[n, d - 1], at_x(d)).wait_recv()
            total = sx[n, xx].astype(F32)
            for d in range(3):
                total += r1x[n, d].astype(F32)
            s2x[n] = total.astype(BF16)
        n = it * 2
        put(s2x.at[n], r2x.at[zi, 2 * tp], x2s.at[n], x2r.at[zi, 2 * tp], at_y(1 + 2 * tp)).start()

        @pl.when(tp == 0)
        def _():
            put(s2x.at[n + 1], r2x.at[zi, 1], x2s.at[n + 1], x2r.at[zi, 1], at_y(2)).start()

    def y_first(zi):
        for d in range(3):
            put(sy.at[0], r1y.at[zi, d], y1s.at[0], y1r.at[zi, d], at_y(d + 1)).wait_recv()
        for x in range(4):
            total = sy[zi * 4 + 3, x].astype(F32)
            for d in range(3):
                total += r1y[zi, d, x].astype(F32)
            s2y[zi, x] = total.astype(BF16)
        for d in range(1, 4):
            put(s2y.at[zi, (xx + d) % 4], r2y.at[zi, d - 1], y2s.at[zi, d - 1], y2r.at[zi, d - 1], at_x(d)).start()

    def second(zi):
        for d in range(3):
            put(s2x.at[0], r2x.at[zi, d], x2s.at[0], x2r.at[zi, d], at_y(d + 1)).wait_recv()
        for d in range(3):
            put(s2y.at[0, 0], r2y.at[zi, d], y2s.at[0, 0], y2r.at[zi, d], at_x(d + 1)).wait_recv()
        upper = s2x[zi * 4 + 3].astype(F32)
        lower = s2y[zi, xx].astype(F32)
        for d in range(3):
            upper += r2x[zi, d].astype(F32)
            lower += r2y[zi, d].astype(F32)
        turned = jnp.concatenate([upper, lower], axis=0).T
        s3[zi, 0] = turned[0:64]
        s3[zi, 1] = turned[64:128]
        zt = (zh + 1 + zi) % 4
        for l in range(2):
            dst = zt * 2 + l
            dist = (dst - zz + 8) % 8

            @pl.when(dist != 0)
            def _():
                put(s3.at[zi, l], r3.at[dist - 1], zs.at[zi, l], zr.at[dist - 1], at_z(dst)).start()

    def visc_second():
        for d in range(1, 4):
            put(v1.at[0], rv1.at[d - 1], v1s.at[d - 1], v1r.at[d - 1], at_y(d)).wait_recv()
        v2[...] = v1[yy] + rv1[0] + rv1[1] + rv1[2]
        for d in range(1, 4):
            put(v2, rv2.at[d - 1], v2s.at[d - 1], v2r.at[d - 1], at_x(d)).start()

    def visc_third():
        for d in range(1, 4):
            put(v2, rv2.at[d - 1], v2s.at[d - 1], v2r.at[d - 1], at_x(d)).wait_recv()
        v3[...] = v2[...] + rv2[0] + rv2[1] + rv2[2]
        for d in range(1, 8):
            z = (zz + d) % 8
            put(v3.at[z // 2], rv3.at[d - 1], v3s.at[d - 1], v3r.at[d - 1], at_z(z)).start()

    def step(it, _):
        products(it, 0)
        for bz in range(1, 4):
            products(it, bz)
            project(bz - 1)
        project(3)
        send_first(it)

        @pl.when(it >= 1)
        def _():
            x_first(it - 1)

        @pl.when((it >= 2) & (it % 2 == 0))
        def _():
            y_first(it // 2 - 1)

        @pl.when((it >= 3) & (it % 2 == 1))
        def _():
            second(it // 2 - 1)

        @pl.when(it < 2)
        def _():
            viscous(it)

        @pl.when(it == 1)
        def _():
            visc_pair().start()

        @pl.when(it == 3)
        def _():
            visc_first()

        @pl.when(it == 4)
        def _():
            visc_second()

        @pl.when(it == 5)
        def _():
            visc_third()

        return 0

    lax.fori_loop(0, 8, step, 0)
    x_first(7)
    y_first(3)
    second(3)

    points = 131072.0
    vtotal = v3[zh]
    for d in range(1, 8):
        put(v3.at[0], rv3.at[d - 1], v3s.at[d - 1], v3r.at[d - 1], partner).wait_recv()
        vtotal += rv3[d - 1]
    lane8 = lax.broadcasted_iota(jnp.int32, (8, 128), 1)
    own = jnp.take_along_axis(vtotal, (lane8 + 8 * gy) % 128, axis=1)
    visc_ref[...] = own[:, 0:8] * (-1.0 / points)
    total = s3[3, zl]
    for d in range(1, 8):
        put(s3.at[0, 0], r3.at[d - 1], zs.at[0, 0], zr.at[d - 1], partner).wait_recv()
        total += r3[d - 1]
    conv_ref[...] = total

    for copy in halo:
        copy.wait_send()
    visc_pair().wait_send()
    for d in range(3):
        put(v1.at[0], rv1.at[d], v1s.at[d], v1r.at[d], partner).wait_send()
        put(v2, rv2.at[d], v2s.at[d], v2r.at[d], partner).wait_send()
    for d in range(7):
        put(v3.at[0], rv3.at[d], v3s.at[d], v3r.at[d], partner).wait_send()

    def sent(zi, _):
        for t in range(4):
            n = zi * 4 + t
            for d in range(3):
                put(sx.at[n, 0], r1x.at[n, d], x1s.at[n, d], x1r.at[n, d], partner).wait_send()
            if t < 3:
                put(sy.at[n], r1y.at[zi, t], y1s.at[n], y1r.at[zi, t], partner).wait_send()
                put(s2x.at[n], r2x.at[zi, t], x2s.at[n], x2r.at[zi, t], partner).wait_send()
        for d in range(3):
            put(s2y.at[zi, 0], r2y.at[zi, d], y2s.at[zi, d], y2r.at[zi, d], partner).wait_send()
        zt = (zh + 1 + zi) % 4
        for l in range(2):

            @pl.when(zt * 2 + l != zz)
            def _():
                put(s3.at[zi, l], r3.at[0], zs.at[zi, l], zr.at[0], partner).wait_send()

        return 0

    lax.fori_loop(0, 4, sent, 0)


def body(modes):
    slabs = modes.transpose(2, 3, 0, 1, 4).reshape(6, 8, 32, 128)
    stencil = jnp.asarray(stencil_matrix(), BF16)
    edges = jnp.asarray(edge_matrix(), BF16)
    eye = jnp.asarray(np.eye(128, dtype=np.float32), BF16)
    dma = pltpu.SemaphoreType.DMA
    vmem = pltpu.VMEM
    conv, visc = pl.pallas_call(
        kernel,
        out_shape=(
            jax.ShapeDtypeStruct((64, 128), F32),
            jax.ShapeDtypeStruct((8, 8), F32),
        ),
        in_specs=[pl.BlockSpec(memory_space=pl.ANY)] * 4,
        out_specs=(pl.BlockSpec(memory_space=vmem),) * 2,
        scratch_shapes=[
            vmem((512, 384), BF16),
            vmem((64, 256), BF16),
            vmem((128, 128), BF16),
            vmem((2, 6, 12, 32, 128), BF16),
            vmem((2, 6, 32, 128), BF16),
            vmem((4, 3, 256, 128), F32),
            vmem((4, 128, 768), BF16),
            vmem((4, 3, 3, 256, 128), BF16),
            vmem((4, 3, 3, 256, 512), F32),
            vmem((768, 1024), BF16),
            vmem((768, 1024), BF16),
            vmem((128, 1024), F32),
            vmem((128, 128), F32),
            vmem((16, 4, 64, 128), BF16),
            vmem((16, 4, 64, 128), BF16),
            vmem((16, 64, 128), BF16),
            vmem((4, 4, 64, 128), BF16),
            vmem((4, 2, 64, 128), F32),
            vmem((16, 3, 64, 128), BF16),
            vmem((4, 3, 4, 64, 128), BF16),
            vmem((4, 3, 64, 128), BF16),
            vmem((4, 3, 64, 128), BF16),
            vmem((7, 64, 128), F32),
            vmem((4, 4, 8, 128), F32),
            vmem((4, 8, 128), F32),
            vmem((4, 8, 128), F32),
            vmem((3, 4, 8, 128), F32),
            vmem((3, 4, 8, 128), F32),
            vmem((7, 8, 128), F32),
            dma((8,)), dma((8,)),
            dma((16, 3)), dma((16, 3)),
            dma((16,)), dma((4, 3)),
            dma((16,)), dma((4, 3)),
            dma((4, 3)), dma((4, 3)),
            dma((4, 2)), dma((7,)),
            dma((3,)), dma((3,)),
            dma((3,)), dma((3,)),
            dma((7,)), dma((7,)),
            dma((4,)),
            vmem((128, 128), F32),
            dma((1,)), dma((1,)),
            vmem((128, 256), BF16),
        ],
        compiler_params=pltpu.CompilerParams(
            collective_id=0, has_side_effects=True, vmem_limit_bytes=60 * 2**20
        ),
    )(slabs, stencil, edges, eye)
    return conv.reshape(8, 8, 128) * (-1.0 / math.sqrt(131072.0)), visc


def solution(mesh):
    in_specs = (P("gx", "gy", None, None, None),)
    out_specs = (P("gx", "gy", None), P("gx", "gy"))
    return jax.shard_map(body, mesh=mesh, in_specs=in_specs, out_specs=out_specs, check_vma=False)
```

```python
import functools
import math

import jax
import jax.numpy as jnp
import numpy as np
from jax import lax
from jax.experimental import pallas as pl
from jax.experimental.pallas import tpu as pltpu
from jax.sharding import PartitionSpec as P

F32 = jnp.float32
BF16 = jnp.bfloat16
MESH = pl.DeviceIdType.MESH

ROWS = 16


def stencil_matrix():
    def column(x, y):
        if x < 0:
            return 256 + (x + 2) * 16 + y
        if x > 15:
            return 288 + (x - 16) * 16 + y
        if y < 0:
            return 320 + x * 2 + y + 2
        if y > 15:
            return 352 + x * 2 + y - 16
        return x * 16 + y

    mat = np.zeros((512, 384), np.float32)
    for x in range(16):
        for y in range(16):
            for off, w in ((1, 8.0), (-1, -8.0), (2, -1.0), (-2, 1.0)):
                mat[x * 16 + y, column(x + off, y)] = w
                mat[256 + x * 16 + y, column(x, y + off)] = w
    return mat


def edge_matrix():
    mat = np.zeros((64, 256), np.float32)
    for side in range(2):
        for x in range(16):
            for l in range(2):
                mat[side * 32 + x * 2 + l, x * 16 + 14 * side + l] = 1.0
    return mat


def kernel(
    m_hbm, d_hbm, e_hbm, i_hbm, conv_ref, visc_ref,
    d_ref, e_ref, i_ref, ext, ed, mf, mt, gbf, gt, w0, w1, acc, vacc,
    sx, sy, s2x, s2y, s3, r1x, r1y, r2x, r2y, r3,
    v1, v2, v3, rv1, rv2, rv3,
    hs, hr, x1s, x1r, y1s, y1r, x2s, x2r, y2s, y2r, zs, zr,
    v1s, v1r, v2s, v2r, v3s, v3r, ins, rv0, v0s, v0r, pick,
):
    gx, gy = lax.axis_index("gx"), lax.axis_index("gy")
    zh, yy = gx // 4, gx % 4
    zl, xx, cc = gy // 8, (gy // 2) % 4, gy % 2
    chip = gy // 2
    zz = zh * 2 + zl
    other = 1 - cc

    def at_x(d):
        return (gx, zl * 8 + ((xx + d) % 4) * 2 + cc)

    def at_y(d):
        return (zh * 4 + (yy + d) % 4, gy)

    def at_z(z):
        return ((z // 2) * 4 + yy, (z % 2) * 8 + xx * 2 + cc)

    def chip_core(step, core):
        return (gx, ((chip + 8 + step) % 8) * 2 + core)

    def row_core(step, core):
        return ((gx + 16 + step) % 16, chip * 2 + core)

    def put(src, dst, send, recv, dev):
        return pltpu.make_async_remote_copy(
            src_ref=src, dst_ref=dst, send_sem=send, recv_sem=recv,
            device_id=dev, device_id_type=MESH,
        )

    barrier = pltpu.get_barrier_semaphore()
    peers = [(gx, chip * 2 + other)]
    for core in range(2):
        for step in (-1, 1):
            peers.append(chip_core(step, core))
            peers.append(row_core(step, core))
    for d in range(1, 4):
        peers.append(at_x(d))
        peers.append(at_y(d))
    for d in range(1, 8):
        peers.append(at_z((zz + d) % 8))
    for dev in peers:
        pl.semaphore_signal(barrier, inc=1, device_id=dev, device_id_type=MESH)

    loads = [
        pltpu.make_async_copy(m_hbm, ext.at[cc, :, 0:8], ins.at[0]),
        pltpu.make_async_copy(e_hbm, e_ref, ins.at[1]),
        pltpu.make_async_copy(i_hbm, i_ref, ins.at[2]),
        pltpu.make_async_copy(d_hbm, d_ref, ins.at[3]),
    ]
    for copy in loads:
        copy.start()
    loads[1].wait()
    loads[0].wait()
    for za in range(6):
        slab = ext[cc, za, 0:8].reshape(256, 128)
        edges = jnp.dot(e_ref[...], slab, preferred_element_type=F32).astype(BF16)
        ed[0, za] = edges[0:32]
        ed[1, za] = edges[32:64]
    for za in range(6):
        ext[other, za, 10 + cc] = ed[other, za]
    pl.semaphore_wait(barrier, len(peers))

    partner = (gx, chip * 2 + other)
    mine = ext.at[cc, :, 0:8]
    last, first = ext.at[cc, :, 7], ext.at[cc, :, 0]
    halo = [
        put(mine, ext.at[cc, :, 0:8], hs.at[0], hr.at[0], partner),
        put(ed.at[other], ext.at[other, :, 10 + cc], hs.at[1], hr.at[1], partner),
    ]
    for core in range(2):
        halo.append(put(last, ext.at[cc, :, 8], hs.at[2 + core], hr.at[2 + cc], row_core(1, core)))
        halo.append(put(first, ext.at[cc, :, 9], hs.at[4 + core], hr.at[4 + cc], row_core(-1, core)))
        halo.append(
            put(ed.at[cc], ext.at[other, :, 11 - cc], hs.at[6 + core], hr.at[6 + cc], chip_core(2 * cc - 1, core))
        )
    for copy in halo:
        copy.start()

    lane = lax.broadcasted_iota(jnp.int32, (32, 128), 1)
    mode_of = [16 * ((lane // 64) * 4 + x) + 8 * cc + lane % 8 for x in range(4)]
    row128 = lax.broadcasted_iota(jnp.int32, (128, 128), 0)
    lane128 = lax.broadcasted_iota(jnp.int32, (128, 128), 1)
    for x in range(2):
        wanted = 16 * ((lane128 // 64) * 4 + x) + 8 * cc + lane128 % 8
        pick[:, x * 128 : x * 128 + 128] = jnp.where(row128 == wanted, 1.0, 0.0).astype(BF16)

    def expand(bz, b, a):
        gt[bz, b, a, :, 0:256] = jnp.dot(gbf[bz, b, a], pick[...], preferred_element_type=F32)
        for p in range(0, 256, 32):
            part = gbf[bz, b, a, p : p + 32].astype(F32)
            for x in range(2, 4):
                gt[bz, b, a, p : p + 32, x * 128 : x * 128 + 128] = jnp.take_along_axis(
                    part, mode_of[x], axis=1
                )

    def inner(blk):
        def one(z, _):
            bz = blk * 2 + z
            sign = (1 - 2 * z).astype(F32) * (8.0 / 12.0)
            for a in range(3):
                slab = ext[blk, z * 3 + a, 0:8].reshape(256, 128)
                mf[bz, a] = slab.astype(F32)
                mt[bz, :, a * 256 : a * 256 + 256] = lax.dot_general(
                    i_ref[...], slab, (((1,), (1,)), ((), ())), preferred_element_type=F32
                ).astype(BF16)
                along_z = ext[blk, (1 - z) * 3 + a, 0:8].reshape(256, 128).astype(F32) * sign
                gbf[bz, 2, a] = along_z.astype(BF16)
            for a in range(3):
                expand(bz, 2, a)
            return 0

        lax.fori_loop(0, 2, one, 0)

    def outer(blk):
        def one(z, _):
            bz = blk * 2 + z
            for a in range(3):
                whole = ext[blk, z * 3 + a].reshape(384, 128)
                both = jnp.dot(d_ref[...], whole, preferred_element_type=F32) * (1.0 / 12.0)
                gbf[bz, 0, a] = both[0:256].astype(BF16)
                gbf[bz, 1, a] = both[256:512].astype(BF16)
            for a in range(3):
                for b in range(2):
                    expand(bz, b, a)
            return 0

        lax.fori_loop(0, 2, one, 0)

    def rows_in(blk):
        put(last, ext.at[blk, :, 8], hs.at[2], hr.at[2 + blk], partner).wait_recv()
        put(first, ext.at[blk, :, 9], hs.at[4], hr.at[4 + blk], partner).wait_recv()
        put(ed.at[0], ext.at[blk, :, 10 + blk], hs.at[6], hr.at[7 - blk], partner).wait_recv()

    loads[2].wait()
    inner(cc)
    put(mine, ext.at[other, :, 0:8], hs.at[0], hr.at[0], partner).wait_recv()
    inner(other)
    loads[3].wait()
    put(ed.at[cc], ext.at[cc, :, 10 + other], hs.at[1], hr.at[1], partner).wait_recv()
    rows_in(cc)
    outer(cc)
    rows_in(other)
    outer(other)

    vacc[...] = jnp.zeros_like(vacc)

    def viscous(it):
        bz = cc * 2 + it
        total = vacc[...]
        for b in range(3):
            for a in range(3):
                g = gbf[bz, b, a]
                total += lax.dot_general(g, g, (((0,), (0,)), ((), ())), preferred_element_type=F32)
        vacc[...] = total

    def visc_pair():
        return put(vacc, rv0, v0s.at[0], v0r.at[0], partner)

    def visc_first():
        visc_pair().wait_recv()
        for h in range(4):
            for y in range(4):
                rows = slice((h * 4 + y) * 8, (h * 4 + y) * 8 + 8)
                v1[y, h] = vacc[rows, :] + rv0[rows, :]
        for d in range(1, 4):
            put(v1.at[(yy + d) % 4], rv1.at[d - 1], v1s.at[d - 1], v1r.at[d - 1], at_y(d)).start()

    ws = (w0, w1)
    lane16 = lax.broadcasted_iota(jnp.int32, (16, 128), 1)

    def products(it, bz):
        zi, tp = it // 2, it % 2
        zt = (zh + 1 + zi) % 4
        idx = [
            (lane16 % 64) // 8 + 8 * (zt * 4 + (yy + 1 + 2 * tp + e) % 4) for e in range(2)
        ]
        w = ws[bz % 2]
        for p in range(0, 256, 16):
            left = [
                [jnp.take_along_axis(mf[bz, a, p : p + 16], idx[e], axis=1) for a in range(3)]
                for e in range(2)
            ]
            for b in range(3):
                for x in range(4):
                    g = [gt[bz, b, a, p : p + 16, x * 128 : x * 128 + 128] for a in range(3)]
                    pair = [
                        left[e][0] * g[0] + left[e][1] * g[1] + left[e][2] * g[2] for e in range(2)
                    ]
                    w[b * 256 + p : b * 256 + p + 16, x * 256 : x * 256 + 256] = jnp.concatenate(
                        pair, axis=1
                    ).astype(BF16)

    def project(bz):
        w = ws[bz % 2]
        for x in range(4):
            cols = slice(x * 256, x * 256 + 256)
            term = jnp.dot(mt[bz], w[:, cols], preferred_element_type=F32)
            if bz == 0:
                acc[:, cols] = term
            else:
                acc[:, cols] += term

    def send_first(it):
        for e in range(2):
            n = it * 2 + e
            for x in range(4):
                tile = acc[:, x * 256 + e * 128 : x * 256 + e * 128 + 128].astype(BF16)
                sx[it, x, e] = tile[0:64]
                sy[n, x] = tile[64:128]
        for d in range(1, 4):
            put(sx.at[it, (xx + d) % 4], r1x.at[it, d - 1], x1s.at[it, d - 1], x1r.at[it, d - 1], at_x(d)).start()
        zi, tp = it // 2, it % 2
        n = it * 2
        put(sy.at[n], r1y.at[zi, 2 * tp], y1s.at[n], y1r.at[zi, 2 * tp], at_y(1 + 2 * tp)).start()

        @pl.when(tp == 0)
        def _():
            put(sy.at[n + 1], r1y.at[zi, 1], y1s.at[n + 1], y1r.at[zi, 1], at_y(2)).start()

    def x_first(it):
        zi, tp = it // 2, it % 2
        for d in range(1, 4):
            put(sx.at[it, 0], r1x.at[it, d - 1], x1s.at[it, d - 1], x1r.at[it, d - 1], at_x(d)).wait_recv()
        for e in range(2):
            total = sx[it, xx, e].astype(F32)
            for d in range(3):
                total += r1x[it, d, e].astype(F32)
            s2x[it * 2 + e] = total.astype(BF16)
        n = it * 2
        put(s2x.at[n], r2x.at[zi, 2 * tp], x2s.at[n], x2r.at[zi, 2 * tp], at_y(1 + 2 * tp)).start()

        @pl.when(tp == 0)
        def _():
            put(s2x.at[n + 1], r2x.at[zi, 1], x2s.at[n + 1], x2r.at[zi, 1], at_y(2)).start()

    def y_first(zi):
        for d in range(3):
            put(sy.at[0], r1y.at[zi, d], y1s.at[0], y1r.at[zi, d], at_y(d + 1)).wait_recv()
        for x in range(4):
            total = sy[zi * 4 + 3, x].astype(F32)
            for d in range(3):
                total += r1y[zi, d, x].astype(F32)
            s2y[zi, x] = total.astype(BF16)
        for d in range(1, 4):
            put(s2y.at[zi, (xx + d) % 4], r2y.at[zi, d - 1], y2s.at[zi, d - 1], y2r.at[zi, d - 1], at_x(d)).start()

    def second(zi):
        for d in range(3):
            put(s2x.at[0], r2x.at[zi, d], x2s.at[0], x2r.at[zi, d], at_y(d + 1)).wait_recv()
        for d in range(3):
            put(s2y.at[0, 0], r2y.at[zi, d], y2s.at[0, 0], y2r.at[zi, d], at_x(d + 1)).wait_recv()
        upper = s2x[zi * 4 + 3].astype(F32)
        lower = s2y[zi, xx].astype(F32)
        for d in range(3):
            upper += r2x[zi, d].astype(F32)
            lower += r2y[zi, d].astype(F32)
        turned = jnp.concatenate([upper, lower], axis=0).T
        s3[zi, 0] = turned[0:64]
        s3[zi, 1] = turned[64:128]
        zt = (zh + 1 + zi) % 4
        for l in range(2):
            dst = zt * 2 + l
            dist = (dst - zz + 8) % 8

            @pl.when(dist != 0)
            def _():
                put(s3.at[zi, l], r3.at[dist - 1], zs.at[zi, l], zr.at[dist - 1], at_z(dst)).start()

    def visc_second():
        for d in range(1, 4):
            put(v1.at[0], rv1.at[d - 1], v1s.at[d - 1], v1r.at[d - 1], at_y(d)).wait_recv()
        v2[...] = v1[yy] + rv1[0] + rv1[1] + rv1[2]
        for d in range(1, 4):
            put(v2, rv2.at[d - 1], v2s.at[d - 1], v2r.at[d - 1], at_x(d)).start()

    def visc_third():
        for d in range(1, 4):
            put(v2, rv2.at[d - 1], v2s.at[d - 1], v2r.at[d - 1], at_x(d)).wait_recv()
        v3[...] = v2[...] + rv2[0] + rv2[1] + rv2[2]
        for d in range(1, 8):
            z = (zz + d) % 8
            put(v3.at[z // 2], rv3.at[d - 1], v3s.at[d - 1], v3r.at[d - 1], at_z(z)).start()

    def step(it, _):
        products(it, 0)
        for bz in range(1, 4):
            products(it, bz)
            project(bz - 1)
        project(3)
        send_first(it)

        @pl.when(it >= 1)
        def _():
            x_first(it - 1)

        @pl.when((it >= 2) & (it % 2 == 0))
        def _():
            y_first(it // 2 - 1)

        @pl.when((it >= 3) & (it % 2 == 1))
        def _():
            second(it // 2 - 1)

        @pl.when(it < 2)
        def _():
            viscous(it)

        @pl.when(it == 1)
        def _():
            visc_pair().start()

        @pl.when(it == 3)
        def _():
            visc_first()

        @pl.when(it == 4)
        def _():
            visc_second()

        @pl.when(it == 5)
        def _():
            visc_third()

        return 0

    lax.fori_loop(0, 8, step, 0)
    x_first(7)
    y_first(3)
    second(3)

    vtotal = v3[zh]
    for d in range(1, 8):
        put(v3.at[0], rv3.at[d - 1], v3s.at[d - 1], v3r.at[d - 1], partner).wait_recv()
        vtotal += rv3[d - 1]
    lane8 = lax.broadcasted_iota(jnp.int32, (8, 128), 1)
    own = jnp.take_along_axis(vtotal, (lane8 + 8 * gy) % 128, axis=1)
    visc_ref[...] = own
    total = s3[3, zl]
    for d in range(1, 8):
        put(s3.at[0, 0], r3.at[d - 1], zs.at[0, 0], zr.at[d - 1], partner).wait_recv()
        total += r3[d - 1]
    conv_ref[...] = total

    for copy in halo:
        copy.wait_send()
    visc_pair().wait_send()
    for d in range(3):
        put(v1.at[0], rv1.at[d], v1s.at[d], v1r.at[d], partner).wait_send()
        put(v2, rv2.at[d], v2s.at[d], v2r.at[d], partner).wait_send()
    for d in range(7):
        put(v3.at[0], rv3.at[d], v3s.at[d], v3r.at[d], partner).wait_send()

    def sent(zi, _):
        for t in range(4):
            n = zi * 4 + t
            if t < 3:
                put(sy.at[n], r1y.at[zi, t], y1s.at[n], y1r.at[zi, t], partner).wait_send()
                put(s2x.at[n], r2x.at[zi, t], x2s.at[n], x2r.at[zi, t], partner).wait_send()
        for d in range(3):
            put(s2y.at[zi, 0], r2y.at[zi, d], y2s.at[zi, d], y2r.at[zi, d], partner).wait_send()
        zt = (zh + 1 + zi) % 4
        for l in range(2):

            @pl.when(zt * 2 + l != zz)
            def _():
                put(s3.at[zi, l], r3.at[0], zs.at[zi, l], zr.at[0], partner).wait_send()

        return 0

    lax.fori_loop(0, 4, sent, 0)

    def sent_x(it, _):
        for d in range(3):
            put(sx.at[it, 0], r1x.at[it, d], x1s.at[it, d], x1r.at[it, d], partner).wait_send()
        return 0

    lax.fori_loop(0, 8, sent_x, 0)


def finish(conv_in, visc_in, conv_ref, visc_ref):
    conv_ref[...] = (conv_in[...] * (-1.0 / math.sqrt(131072.0))).reshape(8, 8, 128)
    visc_ref[...] = visc_in[...][:, 0:8] * (-1.0 / 131072.0)


def body(modes):
    slabs = modes.transpose(2, 3, 0, 1, 4).reshape(6, 8, 32, 128)
    stencil = jnp.asarray(stencil_matrix(), BF16)
    edges = jnp.asarray(edge_matrix(), BF16)
    eye = jnp.asarray(np.eye(128, dtype=np.float32), BF16)
    dma = pltpu.SemaphoreType.DMA
    vmem = pltpu.VMEM
    conv, visc = pl.pallas_call(
        kernel,
        out_shape=(
            jax.ShapeDtypeStruct((64, 128), F32),
            jax.ShapeDtypeStruct((8, 128), F32),
        ),
        in_specs=[pl.BlockSpec(memory_space=pl.ANY)] * 4,
        out_specs=(pl.BlockSpec(memory_space=vmem),) * 2,
        scratch_shapes=[
            vmem((512, 384), BF16),
            vmem((64, 256), BF16),
            vmem((128, 128), BF16),
            vmem((2, 6, 12, 32, 128), BF16),
            vmem((2, 6, 32, 128), BF16),
            vmem((4, 3, 256, 128), F32),
            vmem((4, 128, 768), BF16),
            vmem((4, 3, 3, 256, 128), BF16),
            vmem((4, 3, 3, 256, 512), F32),
            vmem((768, 1024), BF16),
            vmem((768, 1024), BF16),
            vmem((128, 1024), F32),
            vmem((128, 128), F32),
            vmem((8, 4, 2, 64, 128), BF16),
            vmem((16, 4, 64, 128), BF16),
            vmem((16, 64, 128), BF16),
            vmem((4, 4, 64, 128), BF16),
            vmem((4, 2, 64, 128), F32),
            vmem((8, 3, 2, 64, 128), BF16),
            vmem((4, 3, 4, 64, 128), BF16),
            vmem((4, 3, 64, 128), BF16),
            vmem((4, 3, 64, 128), BF16),
            vmem((7, 64, 128), F32),
            vmem((4, 4, 8, 128), F32),
            vmem((4, 8, 128), F32),
            vmem((4, 8, 128), F32),
            vmem((3, 4, 8, 128), F32),
            vmem((3, 4, 8, 128), F32),
            vmem((7, 8, 128), F32),
            dma((8,)), dma((8,)),
            dma((8, 3)), dma((8, 3)),
            dma((16,)), dma((4, 3)),
            dma((16,)), dma((4, 3)),
            dma((4, 3)), dma((4, 3)),
            dma((4, 2)), dma((7,)),
            dma((3,)), dma((3,)),
            dma((3,)), dma((3,)),
            dma((7,)), dma((7,)),
            dma((4,)),
            vmem((128, 128), F32),
            dma((1,)), dma((1,)),
            vmem((128, 256), BF16),
        ],
        compiler_params=pltpu.CompilerParams(
            collective_id=0, has_side_effects=True, vmem_limit_bytes=60 * 2**20
        ),
    )(slabs, stencil, edges, eye)
    return pl.pallas_call(
        finish,
        out_shape=(
            jax.ShapeDtypeStruct((8, 8, 128), F32),
            jax.ShapeDtypeStruct((8, 8), F32),
        ),
        in_specs=[pl.BlockSpec(memory_space=vmem)] * 2,
        out_specs=(pl.BlockSpec(memory_space=vmem),) * 2,
    )(conv, visc)


def solution(mesh):
    in_specs = (P("gx", "gy", None, None, None),)
    out_specs = (P("gx", "gy", None), P("gx", "gy"))
    return jax.shard_map(body, mesh=mesh, in_specs=in_specs, out_specs=out_specs, check_vma=False)
```

```python
import functools
import math

import jax
import jax.numpy as jnp
import numpy as np
from jax import lax
from jax.experimental import pallas as pl
from jax.experimental.pallas import tpu as pltpu
from jax.sharding import PartitionSpec as P

F32 = jnp.float32
BF16 = jnp.bfloat16
MESH = pl.DeviceIdType.MESH

ROWS = 16


def stencil_matrix():
    def column(x, y):
        if x < 0:
            return 256 + (x + 2) * 16 + y
        if x > 15:
            return 288 + (x - 16) * 16 + y
        if y < 0:
            return 320 + x * 2 + y + 2
        if y > 15:
            return 352 + x * 2 + y - 16
        return x * 16 + y

    mat = np.zeros((512, 384), np.float32)
    for x in range(16):
        for y in range(16):
            for off, w in ((1, 8.0), (-1, -8.0), (2, -1.0), (-2, 1.0)):
                mat[x * 16 + y, column(x + off, y)] = w
                mat[256 + x * 16 + y, column(x, y + off)] = w
    return mat


def edge_matrix():
    mat = np.zeros((64, 256), np.float32)
    for side in range(2):
        for x in range(16):
            for l in range(2):
                mat[side * 32 + x * 2 + l, x * 16 + 14 * side + l] = 1.0
    return mat


def kernel(
    m_hbm, d_hbm, e_hbm, i_hbm, conv_ref, visc_ref,
    d_ref, e_ref, i_ref, ext, ed, mf, mt, gbf, gt, gz, w0, w1, acc, vacc,
    sx, sy, s2x, s2y, s3, r1x, r1y, r2x, r2y, r3,
    v1, v2, v3, rv1, rv2, rv3,
    hs, hr, x1s, x1r, y1s, y1r, x2s, x2r, y2s, y2r, zs, zr,
    v1s, v1r, v2s, v2r, v3s, v3r, ins, rv0, v0s, v0r, pick,
):
    gx, gy = lax.axis_index("gx"), lax.axis_index("gy")
    zh, yy = gx // 4, gx % 4
    zl, xx, cc = gy // 8, (gy // 2) % 4, gy % 2
    chip = gy // 2
    zz = zh * 2 + zl
    other = 1 - cc

    def at_x(d):
        return (gx, zl * 8 + ((xx + d) % 4) * 2 + cc)

    def at_y(d):
        return (zh * 4 + (yy + d) % 4, gy)

    def at_z(z):
        return ((z // 2) * 4 + yy, (z % 2) * 8 + xx * 2 + cc)

    def chip_core(step, core):
        return (gx, ((chip + 8 + step) % 8) * 2 + core)

    def row_core(step, core):
        return ((gx + 16 + step) % 16, chip * 2 + core)

    def put(src, dst, send, recv, dev):
        return pltpu.make_async_remote_copy(
            src_ref=src, dst_ref=dst, send_sem=send, recv_sem=recv,
            device_id=dev, device_id_type=MESH,
        )

    barrier = pltpu.get_barrier_semaphore()
    peers = [(gx, chip * 2 + other)]
    for core in range(2):
        for step in (-1, 1):
            peers.append(chip_core(step, core))
            peers.append(row_core(step, core))
    for d in range(1, 4):
        peers.append(at_x(d))
        peers.append(at_y(d))
    for d in range(1, 8):
        peers.append(at_z((zz + d) % 8))
    for dev in peers:
        pl.semaphore_signal(barrier, inc=1, device_id=dev, device_id_type=MESH)

    loads = [
        pltpu.make_async_copy(m_hbm, ext.at[cc, :, 0:8], ins.at[0]),
        pltpu.make_async_copy(e_hbm, e_ref, ins.at[1]),
        pltpu.make_async_copy(i_hbm, i_ref, ins.at[2]),
        pltpu.make_async_copy(d_hbm, d_ref, ins.at[3]),
    ]
    for copy in loads:
        copy.start()
    loads[1].wait()
    loads[0].wait()
    for za in range(6):
        slab = ext[cc, za, 0:8].reshape(256, 128)
        edges = jnp.dot(e_ref[...], slab, preferred_element_type=F32).astype(BF16)
        ed[0, za] = edges[0:32]
        ed[1, za] = edges[32:64]
    for za in range(6):
        ext[other, za, 10 + cc] = ed[other, za]
    pl.semaphore_wait(barrier, len(peers))

    partner = (gx, chip * 2 + other)
    mine = ext.at[cc, :, 0:8]
    last, first = ext.at[cc, :, 7], ext.at[cc, :, 0]
    halo = [
        put(mine, ext.at[cc, :, 0:8], hs.at[0], hr.at[0], partner),
        put(ed.at[other], ext.at[other, :, 10 + cc], hs.at[1], hr.at[1], partner),
    ]
    for core in range(2):
        halo.append(put(last, ext.at[cc, :, 8], hs.at[2 + core], hr.at[2 + cc], row_core(1, core)))
        halo.append(put(first, ext.at[cc, :, 9], hs.at[4 + core], hr.at[4 + cc], row_core(-1, core)))
        halo.append(
            put(ed.at[cc], ext.at[other, :, 11 - cc], hs.at[6 + core], hr.at[6 + cc], chip_core(2 * cc - 1, core))
        )
    for copy in halo:
        copy.start()

    lane = lax.broadcasted_iota(jnp.int32, (32, 128), 1)
    mode_of = [16 * ((lane // 64) * 4 + x) + 8 * cc + lane % 8 for x in range(4)]
    row128 = lax.broadcasted_iota(jnp.int32, (128, 128), 0)
    lane128 = lax.broadcasted_iota(jnp.int32, (128, 128), 1)
    for x in range(2):
        wanted = 16 * ((lane128 // 64) * 4 + x) + 8 * cc + lane128 % 8
        pick[:, x * 128 : x * 128 + 128] = jnp.where(row128 == wanted, 1.0, 0.0).astype(BF16)

    def expand_z(bz, a):
        gz[bz, a, :, 0:256] = jnp.dot(gbf[bz, 2, a], pick[...], preferred_element_type=F32).astype(BF16)
        for p in range(0, 256, 32):
            part = gbf[bz, 2, a, p : p + 32].astype(F32)
            for x in range(2, 4):
                gz[bz, a, p : p + 32, x * 128 : x * 128 + 128] = jnp.take_along_axis(
                    part, mode_of[x], axis=1
                ).astype(BF16)

    def expand(bz, b, a):
        gt[bz, b, a, :, 0:256] = jnp.dot(gbf[bz, b, a], pick[...], preferred_element_type=F32)
        for p in range(0, 256, 32):
            part = gbf[bz, b, a, p : p + 32].astype(F32)
            for x in range(2, 4):
                gt[bz, b, a, p : p + 32, x * 128 : x * 128 + 128] = jnp.take_along_axis(
                    part, mode_of[x], axis=1
                )

    def inner(blk):
        def one(z, _):
            bz = blk * 2 + z
            sign = (1 - 2 * z).astype(F32) * (8.0 / 12.0)
            for a in range(3):
                slab = ext[blk, z * 3 + a, 0:8].reshape(256, 128)
                mf[bz, a] = slab.astype(F32)
                mt[bz, :, a * 256 : a * 256 + 256] = lax.dot_general(
                    i_ref[...], slab, (((1,), (1,)), ((), ())), preferred_element_type=F32
                ).astype(BF16)
                along_z = ext[blk, (1 - z) * 3 + a, 0:8].reshape(256, 128).astype(F32) * sign
                gbf[bz, 2, a] = along_z.astype(BF16)
            for a in range(3):
                expand_z(bz, a)
            return 0

        lax.fori_loop(0, 2, one, 0)

    def outer(blk):
        def one(z, _):
            bz = blk * 2 + z
            for a in range(3):
                whole = ext[blk, z * 3 + a].reshape(384, 128)
                both = jnp.dot(d_ref[...], whole, preferred_element_type=F32) * (1.0 / 12.0)
                gbf[bz, 0, a] = both[0:256].astype(BF16)
                gbf[bz, 1, a] = both[256:512].astype(BF16)
            for a in range(3):
                for b in range(2):
                    expand(bz, b, a)
            return 0

        lax.fori_loop(0, 2, one, 0)

    def rows_in(blk):
        put(last, ext.at[blk, :, 8], hs.at[2], hr.at[2 + blk], partner).wait_recv()
        put(first, ext.at[blk, :, 9], hs.at[4], hr.at[4 + blk], partner).wait_recv()
        put(ed.at[0], ext.at[blk, :, 10 + blk], hs.at[6], hr.at[7 - blk], partner).wait_recv()

    loads[2].wait()
    inner(cc)
    put(mine, ext.at[other, :, 0:8], hs.at[0], hr.at[0], partner).wait_recv()
    inner(other)
    loads[3].wait()
    put(ed.at[cc], ext.at[cc, :, 10 + other], hs.at[1], hr.at[1], partner).wait_recv()
    rows_in(cc)
    outer(cc)
    rows_in(other)
    outer(other)

    vacc[...] = jnp.zeros_like(vacc)

    def viscous(it):
        bz = cc * 2 + it
        total = vacc[...]
        for b in range(3):
            for a in range(3):
                g = gbf[bz, b, a]
                total += lax.dot_general(g, g, (((0,), (0,)), ((), ())), preferred_element_type=F32)
        vacc[...] = total

    def visc_pair():
        return put(vacc, rv0, v0s.at[0], v0r.at[0], partner)

    def visc_first():
        visc_pair().wait_recv()
        for h in range(4):
            for y in range(4):
                rows = slice((h * 4 + y) * 8, (h * 4 + y) * 8 + 8)
                v1[y, h] = vacc[rows, :] + rv0[rows, :]
        for d in range(1, 4):
            put(v1.at[(yy + d) % 4], rv1.at[d - 1], v1s.at[d - 1], v1r.at[d - 1], at_y(d)).start()

    ws = (w0, w1)
    lane16 = lax.broadcasted_iota(jnp.int32, (16, 128), 1)

    def products(it, bz):
        zi, tp = it // 2, it % 2
        zt = (zh + 1 + zi) % 4
        idx = [
            (lane16 % 64) // 8 + 8 * (zt * 4 + (yy + 1 + 2 * tp + e) % 4) for e in range(2)
        ]
        w = ws[bz % 2]
        for p in range(0, 256, 16):
            left = [
                [jnp.take_along_axis(mf[bz, a, p : p + 16], idx[e], axis=1) for a in range(3)]
                for e in range(2)
            ]
            for b in range(2):
                for x in range(4):
                    g = [gt[bz, b, a, p : p + 16, x * 128 : x * 128 + 128] for a in range(3)]
                    pair = [
                        left[e][0] * g[0] + left[e][1] * g[1] + left[e][2] * g[2] for e in range(2)
                    ]
                    w[b * 256 + p : b * 256 + p + 16, x * 256 : x * 256 + 256] = jnp.concatenate(
                        pair, axis=1
                    ).astype(BF16)
            short = [[factor.astype(BF16) for factor in row] for row in left]
            for x in range(4):
                g = [gz[bz, a, p : p + 16, x * 128 : x * 128 + 128] for a in range(3)]
                pair = [
                    short[e][0] * g[0] + short[e][1] * g[1] + short[e][2] * g[2] for e in range(2)
                ]
                w[512 + p : 512 + p + 16, x * 256 : x * 256 + 256] = jnp.concatenate(pair, axis=1)

    def project(bz):
        w = ws[bz % 2]
        for x in range(4):
            cols = slice(x * 256, x * 256 + 256)
            term = jnp.dot(mt[bz], w[:, cols], preferred_element_type=F32)
            if bz == 0:
                acc[:, cols] = term
            else:
                acc[:, cols] += term

    def send_first(it):
        for e in range(2):
            n = it * 2 + e
            for x in range(4):
                tile = acc[:, x * 256 + e * 128 : x * 256 + e * 128 + 128].astype(BF16)
                sx[it, x, e] = tile[0:64]
                sy[n, x] = tile[64:128]
        for d in range(1, 4):
            put(sx.at[it, (xx + d) % 4], r1x.at[it, d - 1], x1s.at[it, d - 1], x1r.at[it, d - 1], at_x(d)).start()
        zi, tp = it // 2, it % 2
        n = it * 2
        put(sy.at[n], r1y.at[zi, 2 * tp], y1s.at[n], y1r.at[zi, 2 * tp], at_y(1 + 2 * tp)).start()

        @pl.when(tp == 0)
        def _():
            put(sy.at[n + 1], r1y.at[zi, 1], y1s.at[n + 1], y1r.at[zi, 1], at_y(2)).start()

    def x_first(it):
        zi, tp = it // 2, it % 2
        for d in range(1, 4):
            put(sx.at[it, 0], r1x.at[it, d - 1], x1s.at[it, d - 1], x1r.at[it, d - 1], at_x(d)).wait_recv()
        for e in range(2):
            total = sx[it, xx, e].astype(F32)
            for d in range(3):
                total += r1x[it, d, e].astype(F32)
            s2x[it * 2 + e] = total.astype(BF16)
        n = it * 2
        put(s2x.at[n], r2x.at[zi, 2 * tp], x2s.at[n], x2r.at[zi, 2 * tp], at_y(1 + 2 * tp)).start()

        @pl.when(tp == 0)
        def _():
            put(s2x.at[n + 1], r2x.at[zi, 1], x2s.at[n + 1], x2r.at[zi, 1], at_y(2)).start()

    def y_first(zi):
        for d in range(3):
            put(sy.at[0], r1y.at[zi, d], y1s.at[0], y1r.at[zi, d], at_y(d + 1)).wait_recv()
        for x in range(4):
            total = sy[zi * 4 + 3, x].astype(F32)
            for d in range(3):
                total += r1y[zi, d, x].astype(F32)
            s2y[zi, x] = total.astype(BF16)
        for d in range(1, 4):
            put(s2y.at[zi, (xx + d) % 4], r2y.at[zi, d - 1], y2s.at[zi, d - 1], y2r.at[zi, d - 1], at_x(d)).start()

    def second(zi):
        for d in range(3):
            put(s2x.at[0], r2x.at[zi, d], x2s.at[0], x2r.at[zi, d], at_y(d + 1)).wait_recv()
        for d in range(3):
            put(s2y.at[0, 0], r2y.at[zi, d], y2s.at[0, 0], y2r.at[zi, d], at_x(d + 1)).wait_recv()
        upper = s2x[zi * 4 + 3].astype(F32)
        lower = s2y[zi, xx].astype(F32)
        for d in range(3):
            upper += r2x[zi, d].astype(F32)
            lower += r2y[zi, d].astype(F32)
        turned = jnp.concatenate([upper, lower], axis=0).T
        s3[zi, 0] = turned[0:64]
        s3[zi, 1] = turned[64:128]
        zt = (zh + 1 + zi) % 4
        for l in range(2):
            dst = zt * 2 + l
            dist = (dst - zz + 8) % 8

            @pl.when(dist != 0)
            def _():
                put(s3.at[zi, l], r3.at[dist - 1], zs.at[zi, l], zr.at[dist - 1], at_z(dst)).start()

    def visc_second():
        for d in range(1, 4):
            put(v1.at[0], rv1.at[d - 1], v1s.at[d - 1], v1r.at[d - 1], at_y(d)).wait_recv()
        v2[...] = v1[yy] + rv1[0] + rv1[1] + rv1[2]
        for d in range(1, 4):
            put(v2, rv2.at[d - 1], v2s.at[d - 1], v2r.at[d - 1], at_x(d)).start()

    def visc_third():
        for d in range(1, 4):
            put(v2, rv2.at[d - 1], v2s.at[d - 1], v2r.at[d - 1], at_x(d)).wait_recv()
        v3[...] = v2[...] + rv2[0] + rv2[1] + rv2[2]
        for d in range(1, 8):
            z = (zz + d) % 8
            put(v3.at[z // 2], rv3.at[d - 1], v3s.at[d - 1], v3r.at[d - 1], at_z(z)).start()

    def step(it, _):
        products(it, 0)
        for bz in range(1, 4):
            products(it, bz)
            project(bz - 1)
        project(3)
        send_first(it)

        @pl.when(it >= 1)
        def _():
            x_first(it - 1)

        @pl.when((it >= 2) & (it % 2 == 0))
        def _():
            y_first(it // 2 - 1)

        @pl.when((it >= 3) & (it % 2 == 1))
        def _():
            second(it // 2 - 1)

        @pl.when(it < 2)
        def _():
            viscous(it)

        @pl.when(it == 1)
        def _():
            visc_pair().start()

        @pl.when(it == 3)
        def _():
            visc_first()

        @pl.when(it == 4)
        def _():
            visc_second()

        @pl.when(it == 5)
        def _():
            visc_third()

        return 0

    lax.fori_loop(0, 8, step, 0)
    x_first(7)
    y_first(3)
    second(3)

    vtotal = v3[zh]
    for d in range(1, 8):
        put(v3.at[0], rv3.at[d - 1], v3s.at[d - 1], v3r.at[d - 1], partner).wait_recv()
        vtotal += rv3[d - 1]
    lane8 = lax.broadcasted_iota(jnp.int32, (8, 128), 1)
    own = jnp.take_along_axis(vtotal, (lane8 + 8 * gy) % 128, axis=1)
    visc_ref[...] = own
    total = s3[3, zl]
    for d in range(1, 8):
        put(s3.at[0, 0], r3.at[d - 1], zs.at[0, 0], zr.at[d - 1], partner).wait_recv()
        total += r3[d - 1]
    conv_ref[...] = total

    for copy in halo:
        copy.wait_send()
    visc_pair().wait_send()
    for d in range(3):
        put(v1.at[0], rv1.at[d], v1s.at[d], v1r.at[d], partner).wait_send()
        put(v2, rv2.at[d], v2s.at[d], v2r.at[d], partner).wait_send()
    for d in range(7):
        put(v3.at[0], rv3.at[d], v3s.at[d], v3r.at[d], partner).wait_send()

    def sent(zi, _):
        for t in range(4):
            n = zi * 4 + t
            if t < 3:
                put(sy.at[n], r1y.at[zi, t], y1s.at[n], y1r.at[zi, t], partner).wait_send()
                put(s2x.at[n], r2x.at[zi, t], x2s.at[n], x2r.at[zi, t], partner).wait_send()
        for d in range(3):
            put(s2y.at[zi, 0], r2y.at[zi, d], y2s.at[zi, d], y2r.at[zi, d], partner).wait_send()
        zt = (zh + 1 + zi) % 4
        for l in range(2):

            @pl.when(zt * 2 + l != zz)
            def _():
                put(s3.at[zi, l], r3.at[0], zs.at[zi, l], zr.at[0], partner).wait_send()

        return 0

    lax.fori_loop(0, 4, sent, 0)

    def sent_x(it, _):
        for d in range(3):
            put(sx.at[it, 0], r1x.at[it, d], x1s.at[it, d], x1r.at[it, d], partner).wait_send()
        return 0

    lax.fori_loop(0, 8, sent_x, 0)


def finish(conv_in, visc_in, conv_ref, visc_ref):
    conv_ref[...] = (conv_in[...] * (-1.0 / math.sqrt(131072.0))).reshape(8, 8, 128)
    visc_ref[...] = visc_in[...][:, 0:8] * (-1.0 / 131072.0)


def body(modes):
    slabs = modes.transpose(2, 3, 0, 1, 4).reshape(6, 8, 32, 128)
    stencil = jnp.asarray(stencil_matrix(), BF16)
    edges = jnp.asarray(edge_matrix(), BF16)
    eye = jnp.asarray(np.eye(128, dtype=np.float32), BF16)
    dma = pltpu.SemaphoreType.DMA
    vmem = pltpu.VMEM
    conv, visc = pl.pallas_call(
        kernel,
        out_shape=(
            jax.ShapeDtypeStruct((64, 128), F32),
            jax.ShapeDtypeStruct((8, 128), F32),
        ),
        in_specs=[pl.BlockSpec(memory_space=pl.ANY)] * 4,
        out_specs=(pl.BlockSpec(memory_space=vmem),) * 2,
        scratch_shapes=[
            vmem((512, 384), BF16),
            vmem((64, 256), BF16),
            vmem((128, 128), BF16),
            vmem((2, 6, 12, 32, 128), BF16),
            vmem((2, 6, 32, 128), BF16),
            vmem((4, 3, 256, 128), F32),
            vmem((4, 128, 768), BF16),
            vmem((4, 3, 3, 256, 128), BF16),
            vmem((4, 2, 3, 256, 512), F32),
            vmem((4, 3, 256, 512), BF16),
            vmem((768, 1024), BF16),
            vmem((768, 1024), BF16),
            vmem((128, 1024), F32),
            vmem((128, 128), F32),
            vmem((8, 4, 2, 64, 128), BF16),
            vmem((16, 4, 64, 128), BF16),
            vmem((16, 64, 128), BF16),
            vmem((4, 4, 64, 128), BF16),
            vmem((4, 2, 64, 128), F32),
            vmem((8, 3, 2, 64, 128), BF16),
            vmem((4, 3, 4, 64, 128), BF16),
            vmem((4, 3, 64, 128), BF16),
            vmem((4, 3, 64, 128), BF16),
            vmem((7, 64, 128), F32),
            vmem((4, 4, 8, 128), F32),
            vmem((4, 8, 128), F32),
            vmem((4, 8, 128), F32),
            vmem((3, 4, 8, 128), F32),
            vmem((3, 4, 8, 128), F32),
            vmem((7, 8, 128), F32),
            dma((8,)), dma((8,)),
            dma((8, 3)), dma((8, 3)),
            dma((16,)), dma((4, 3)),
            dma((16,)), dma((4, 3)),
            dma((4, 3)), dma((4, 3)),
            dma((4, 2)), dma((7,)),
            dma((3,)), dma((3,)),
            dma((3,)), dma((3,)),
            dma((7,)), dma((7,)),
            dma((4,)),
            vmem((128, 128), F32),
            dma((1,)), dma((1,)),
            vmem((128, 256), BF16),
        ],
        compiler_params=pltpu.CompilerParams(
            collective_id=0, has_side_effects=True, vmem_limit_bytes=60 * 2**20
        ),
    )(slabs, stencil, edges, eye)
    return pl.pallas_call(
        finish,
        out_shape=(
            jax.ShapeDtypeStruct((8, 8, 128), F32),
            jax.ShapeDtypeStruct((8, 8), F32),
        ),
        in_specs=[pl.BlockSpec(memory_space=vmem)] * 2,
        out_specs=(pl.BlockSpec(memory_space=vmem),) * 2,
    )(conv, visc)


def solution(mesh):
    in_specs = (P("gx", "gy", None, None, None),)
    out_specs = (P("gx", "gy", None), P("gx", "gy"))
    return jax.shard_map(body, mesh=mesh, in_specs=in_specs, out_specs=out_specs, check_vma=False)
```
